32 devices in a mesh: groups: 2 (over y), chan: 4 (over z), space: 2 (over x), pair: 2 (over core).
Axes of the slice: x: 2, y: 2, z: 4, core: 2. Of those that a mesh axis runs over, the one named last changes fastest.
Arguments:
- grad_out: bfloat16 [512, 32, 1024], P('chan', ('groups', 'space', 'pair')), parts along dimension 1, may hold values from -6 to 6
- conv_weight: bfloat16 [27, 512, 512], P(None, 'chan'), may hold values from -0.0546875 to 0.0546875
- pre_act: bfloat16 [32, 1024, 512], P(('groups', 'space', 'pair'), 'chan'), parts along dimension 0, may hold values from -6 to 6
- down_weight: bfloat16 [8, 256, 512], replicated, may hold values from -0.25 to 0.25
Outputs:
- grad_fine: bfloat16 [32, 1024, 8, 256], P(('groups', 'space', 'pair'), 'chan'), parts along dimension 0
The draws below stay inside these ranges and needn't reach their ends.
There are 2 independent parts, one for each index of `groups`. The reference program is written for one: setup_inputs(seed, part) draws one part's arguments, and reference() takes and returns one part's arrays. A program takes and returns all parts, laid end to end along the dimension named above; an argument that names none is the same for every part. Nothing has to cross between parts.
All inputs are finite; a program needn't handle non-finite values.
Results may differ from the reference program's by a relative error of at most 0.025.
Values may be sent and summed in bfloat16 or wider, within the bound.
No kernel may reach another device: no remote copies, remote signals or barrier semaphores. Data moves between devices by JAX's collectives and lax.ppermute only.
A program may use at most 64 MiB of HBM per device.

```python
import math
import jax
import jax.numpy as jnp
from jax import lax

C = 512
CF = 256
NZ = 8
NX = 16
PLANE = 1024
N_CHAN = 4


def block_levels(own_key, shape, split, low, largest):
    def one(axis_at, parts):
        steps = jax.random.uniform(jax.random.fold_in(jax.random.fold_in(own_key, 6), axis_at), (parts,), jnp.float32, low / len(split), largest / len(split))
        return jnp.repeat(jnp.exp(steps), shape[axis_at] // parts).reshape((-1,) + (1,) * (len(shape) - axis_at - 1))

    gain = one(*split[0])
    for cut in split[1:]:
        gain = gain * one(*cut)
    return gain


def noise(rng, shape, width, bound, cuts=(), kind=jnp.bfloat16):
    values = jax.random.normal(rng, shape, jnp.float32) * width
    if len(cuts) > 0:
        values = block_levels(rng, shape, cuts, -0.22, 0.18) * values
    return jnp.clip(values, min=-bound, max=bound).astype(kind)


def setup_inputs(seed: int = 0, part: int = 0) -> dict:
    splits = jax.random.split(jax.random.key(seed), 5)
    part_splits = jax.random.split(jax.random.fold_in(splits[4], part), 5)
    return {
        "grad_out": noise(part_splits[0], (C, NX, PLANE), 1.0, 6.0, ((0, 4), (1, 4))),
        "conv_weight": noise(splits[1], (27, C, C), (27 * C) ** -0.5, 0.0546875, ((1, 4),)),
        "pre_act": noise(part_splits[2], (NX, PLANE, C), 1.5, 6.0, ((0, 4), (1, 4))),
        "down_weight": noise(splits[3], (8, CF, C), C ** -0.5, 0.25),
    }


def shifted_stack(padded, depth):
    extent = padded.shape[1] - 2
    plane_len = padded.shape[2]
    widened = jnp.pad(padded, ((0, 0), (0, 0), (depth + 1, depth + 1)))
    z_index = jnp.arange(plane_len, dtype=jnp.int32) % depth
    pieces = []
    for step_x in (-1, 0, 1):
        x_rows = widened[:, 1 - step_x:1 - step_x + extent, :]
        for step_y in (-1, 0, 1):
            for step_z in (-1, 0, 1):
                offset = step_y * depth + step_z
                piece = x_rows[:, :, depth + 1 - offset:depth + 1 - offset + plane_len]
                inside = (z_index - step_z >= 0) & (z_index - step_z < depth)
                pieces.append(jnp.where(inside, piece, jnp.zeros_like(piece)))
    return jnp.stack(pieces)

def gelu_slope(values):
    return 0.5 * (1.0 + jax.scipy.special.erf(values / math.sqrt(2.0))) + values * jnp.exp(-0.5 * values * values) / math.sqrt(2.0 * math.pi)

def reference(grad_out, conv_weight, pre_act, down_weight):
    extent = grad_out.shape[1]
    padded = jnp.pad(grad_out, ((0, 0), (1, 1), (0, 0)))
    per_block = C // N_CHAN

    def block_term(carry, index):
        start = (index * per_block).astype(jnp.int32)
        block_grad = lax.dynamic_slice_in_dim(padded, start, per_block, 0)
        block_weight = lax.dynamic_slice_in_dim(conv_weight, start, per_block, 1)
        stacked = shifted_stack(block_grad, NZ)
        term = jnp.einsum('dokp,doi->kpi', stacked.astype(jnp.float32), block_weight.astype(jnp.float32))
        term = lax.optimization_barrier(term.astype(jnp.bfloat16)).astype(jnp.float32)
        return (carry + term, None)
    total, unused = lax.scan(block_term, jnp.zeros((extent, PLANE, C), jnp.float32), jnp.arange(N_CHAN, dtype=jnp.int32))
    grad_act = total.astype(jnp.bfloat16)
    values = pre_act.astype(jnp.float32)
    grad_pre = (grad_act.astype(jnp.float32) * gelu_slope(values)).astype(jnp.bfloat16)
    result = jnp.einsum('xpk,efk->xpef', grad_pre.astype(jnp.float32), down_weight.astype(jnp.float32))
    return result.astype(jnp.bfloat16)
```

```python
import math

import jax
import jax.numpy as jnp
from jax import lax
from jax.sharding import PartitionSpec as P

NZ = 8


def with_halo(cells, sides, width):
    for axis, dim in sides:
        count = lax.axis_size(axis)
        ends = count - 1
        head = lax.slice_in_dim(cells, 0, width, axis=dim)
        tail = lax.slice_in_dim(cells, cells.shape[dim] - width, cells.shape[dim], axis=dim)
        cells = jnp.concatenate(
            [
                lax.ppermute(tail, axis, [(i, (i + 1) % count) for i in range(ends)]),
                cells,
                lax.ppermute(head, axis, [((i + 1) % count, i) for i in range(ends)]),
            ],
            axis=dim,
        )
    return cells


def shifted_stack(padded, depth):
    extent = padded.shape[1] - 2
    plane_len = padded.shape[2]
    widened = jnp.pad(padded, ((0, 0), (0, 0), (depth + 1, depth + 1)))
    z_index = jnp.arange(plane_len, dtype=jnp.int32) % depth
    pieces = []
    for step_x in (-1, 0, 1):
        x_rows = widened[:, 1 - step_x : 1 - step_x + extent, :]
        for step_y in (-1, 0, 1):
            for step_z in (-1, 0, 1):
                offset = step_y * depth + step_z
                piece = x_rows[:, :, depth + 1 - offset : depth + 1 - offset + plane_len]
                inside = (z_index - step_z >= 0) & (z_index - step_z < depth)
                pieces.append(jnp.where(inside, piece, jnp.zeros_like(piece)))
    return jnp.stack(pieces)


def gelu_slope(values):
    return 0.5 * (1.0 + jax.scipy.special.erf(values / math.sqrt(2.0))) + values * jnp.exp(
        -0.5 * values * values
    ) / math.sqrt(2.0 * math.pi)


def body(grad_out, conv_weight, pre_act, down_weight):
    padded = with_halo(grad_out, ((("space", "pair"), 1),), 1)
    stacked = shifted_stack(padded, NZ)
    partial_sum = lax.dot_general(
        stacked, conv_weight, (((0, 1), (0, 1)), ((), ())), preferred_element_type=jnp.float32
    )
    grad_act = lax.psum_scatter(
        partial_sum.astype(jnp.bfloat16), "chan", scatter_dimension=1, tiled=True
    )
    values = pre_act.astype(jnp.float32)
    grad_pre = (grad_act.astype(jnp.float32) * gelu_slope(values)).astype(jnp.bfloat16)
    result = lax.dot_general(
        grad_pre, down_weight, (((2,), (2,)), ((), ())), preferred_element_type=jnp.float32
    )
    return result.astype(jnp.bfloat16)


def solution(mesh):
    in_specs = (
        P("chan", ("groups", "space", "pair"), None),
        P(None, "chan", None),
        P(("groups", "space", "pair"), "chan", None),
        P(),
    )
    out_specs = P(("groups", "space", "pair"), "chan", None, None)
    return jax.shard_map(body, mesh=mesh, in_specs=in_specs, out_specs=out_specs, check_vma=False)
```

```python
import functools
import math

import jax
import jax.numpy as jnp
from jax import lax
from jax.experimental import pallas as pl
from jax.experimental.pallas import tpu as pltpu
from jax.sharding import PartitionSpec as P

NZ = 8
PLANAR = ("groups", "space", "pair")
SLAB = ("space", "pair")


def gelu_slope(values):
    return 0.5 * (1.0 + jax.scipy.special.erf(values / math.sqrt(2.0))) + values * jnp.exp(
        -0.5 * values * values
    ) / math.sqrt(2.0 * math.pi)


def with_halo(cells, sides, width):
    for axis, dim in sides:
        count = lax.axis_size(axis)
        ends = count - 1
        head = lax.slice_in_dim(cells, 0, width, axis=dim)
        tail = lax.slice_in_dim(cells, cells.shape[dim] - width, cells.shape[dim], axis=dim)
        cells = jnp.concatenate(
            [
                lax.ppermute(tail, axis, [(i, (i + 1) % count) for i in range(ends)]),
                cells,
                lax.ppermute(head, axis, [((i + 1) % count, i) for i in range(ends)]),
            ],
            axis=dim,
        )
    return cells


def shifted_stack(padded, depth):
    extent = padded.shape[1] - 2
    plane_len = padded.shape[2]
    widened = jnp.pad(padded, ((0, 0), (0, 0), (depth + 1, depth + 1)))
    z_index = jnp.arange(plane_len, dtype=jnp.int32) % depth
    pieces = []
    for step_x in (-1, 0, 1):
        x_rows = widened[:, 1 - step_x : 1 - step_x + extent, :]
        for step_y in (-1, 0, 1):
            for step_z in (-1, 0, 1):
                offset = step_y * depth + step_z
                piece = x_rows[:, :, depth + 1 - offset : depth + 1 - offset + plane_len]
                inside = (z_index - step_z >= 0) & (z_index - step_z < depth)
                pieces.append(jnp.where(inside, piece, jnp.zeros_like(piece)))
    return jnp.stack(pieces)


def general_body(grad_out, conv_weight, pre_act, down_weight):
    padded = with_halo(grad_out, ((SLAB, 1),), 1)
    stacked = shifted_stack(padded, NZ)
    partial_sum = lax.dot_general(
        stacked, conv_weight, (((0, 1), (0, 1)), ((), ())), preferred_element_type=jnp.float32
    )
    owned = lax.psum_scatter(
        partial_sum.astype(jnp.bfloat16), "chan", scatter_dimension=2, tiled=True
    )
    grad_act = lax.all_to_all(owned, "chan", split_axis=1, concat_axis=2, tiled=True)
    values = pre_act.astype(jnp.float32)
    grad_pre = (grad_act.astype(jnp.float32) * gelu_slope(values)).astype(jnp.bfloat16)
    result = lax.dot_general(
        grad_pre, down_weight, (((2,), (2,)), ((), ())), preferred_element_type=jnp.float32
    )
    return result.astype(jnp.bfloat16)


def conv_kernel(where_ref, main_ref, low_ref, high_ref, *refs, pieces, added):
    weights = refs[:pieces]
    start_ref = refs[pieces] if added else None
    out_ref, copies, table, sems = refs[pieces + int(added) :]
    extent = main_ref.shape[1]
    rows = main_ref.shape[2]
    width = main_ref.shape[3]
    cells = rows - 2 * NZ
    share = table.shape[0] // pieces
    if pieces == 1:
        spots = [0]
    else:
        q = where_ref[0]
        first = 2 + 2 * (q & 1)
        second = 6 - first
        spots = [q, q ^ first, q ^ second, q ^ 6, q ^ 1, q ^ 1 ^ second, q ^ 1 ^ first, q ^ 7]
    loads = []
    for n in range(pieces):
        row = spots[n] * share if pieces == 1 else pl.multiple_of(spots[n] * share, 16)
        loads.append(
            pltpu.make_async_copy(weights[n], table.at[pl.ds(row, share), :], sems.at[n])
        )

    @pl.when(pl.program_id(0) == 0)
    def _():
        for load in loads:
            load.start()

    depth_at = lax.broadcasted_iota(jnp.int32, (rows, width), 0) % NZ
    for x in range(extent + 2):
        if x == 0:
            plane = low_ref[0, 0]
        elif x == extent + 1:
            plane = high_ref[0, 0]
        else:
            plane = main_ref[0, x - 1]
        plane = plane.astype(jnp.float32)
        for step_z in (-1, 0, 1):
            if step_z == 1:
                moved = jnp.where(depth_at >= 1, pltpu.roll(plane, 1, 0), 0.0)
            elif step_z == -1:
                moved = jnp.where(depth_at < NZ - 1, pltpu.roll(plane, rows - 1, 0), 0.0)
            else:
                moved = plane
            for step_y in (-1, 0, 1):
                at = NZ * (1 - step_y)
                lane = (3 * (step_y + 1) + step_z + 1) * width
                copies[x, :, lane : lane + width] = moved[at : at + cells].astype(jnp.bfloat16)

    @pl.when(pl.program_id(0) == 0)
    def _():
        for load in loads:
            load.wait()

    total = start_ref[0] if added else None
    for step_x in (-1, 0, 1):
        left = copies[1 - step_x : 1 - step_x + extent].reshape(extent * cells, 9 * width)
        right = table[(step_x + 1) * 9 * width : (step_x + 2) * 9 * width]
        term = jnp.dot(left, right, preferred_element_type=jnp.float32)
        total = term if total is None else total + term
    out_ref[0] = total.astype(out_ref.dtype)


def conv_blocks(where, main, low, high, weights, start, slot, kind):
    count, extent, rows, width = main.shape
    cells = extent * (rows - 2 * NZ)
    wide = weights[0].shape[1]
    table_rows = sum(v.shape[0] for v in weights)
    in_specs = [
        pl.BlockSpec(memory_space=pltpu.SMEM),
        pl.BlockSpec((1, extent, rows, width), lambda i: (i, 0, 0, 0)),
        pl.BlockSpec((1, 1, rows, width), lambda i: (i, 0, 0, 0)),
        pl.BlockSpec((1, 1, rows, width), lambda i: (i, 0, 0, 0)),
    ] + [pl.BlockSpec(memory_space=pl.ANY)] * len(weights)
    operands = [where, main, low, high, *weights]
    if start is not None:
        in_specs.append(pl.BlockSpec((1, cells, wide), lambda i: (slot + i, 0, 0)))
        operands.append(start)
    return pl.pallas_call(
        functools.partial(conv_kernel, pieces=len(weights), added=start is not None),
        grid=(count,),
        in_specs=in_specs,
        out_specs=pl.BlockSpec((1, cells, wide), lambda i: (i, 0, 0)),
        out_shape=jax.ShapeDtypeStruct((count, cells, wide), kind),
        scratch_shapes=[
            pltpu.VMEM((extent + 2, rows - 2 * NZ, 9 * width), jnp.bfloat16),
            pltpu.VMEM((table_rows, wide), jnp.bfloat16),
            pltpu.SemaphoreType.DMA((len(weights),)),
        ],
        compiler_params=pltpu.CompilerParams(vmem_limit_bytes=40 * 2**20),
        cost_estimate=pl.CostEstimate(
            flops=2 * count * cells * table_rows * wide,
            transcendentals=0,
            bytes_accessed=2 * table_rows * wide + count * cells * wide * 6,
        ),
        name="conv_blocks",
    )(*operands)


def down_kernel(mine_ref, theirs_ref, slope_ref, weight_ref, out_ref, spread):
    act = (mine_ref[0] + theirs_ref[0].astype(jnp.float32)).astype(jnp.bfloat16)
    pre = (act.astype(jnp.float32) * slope_ref[0]).astype(jnp.bfloat16)
    cells = pre.shape[0]
    offsets, fine = out_ref.shape[2], out_ref.shape[3]
    lanes = spread.shape[2]
    for e in range(offsets):
        grown = lax.dot_general(
            pre,
            weight_ref[e],
            (((1,), (1,)), ((), ())),
            preferred_element_type=jnp.float32,
        )
        for h in range(fine // lanes):
            spread[h, e * cells : (e + 1) * cells] = grown[:, h * lanes : (h + 1) * lanes]
    for p in range(cells):
        for h in range(fine // lanes):
            out_ref[0, p, :, h * lanes : (h + 1) * lanes] = spread[
                h, pl.ds(p, offsets, stride=cells), :
            ].astype(out_ref.dtype)


def down_blocks(mine, theirs, slope, weight):
    extent, cells, wide = slope.shape
    offsets, fine, _ = weight.shape
    return pl.pallas_call(
        down_kernel,
        grid=(extent,),
        in_specs=[
            pl.BlockSpec((1, cells, wide), lambda i: (i, 0, 0)),
            pl.BlockSpec((1, cells, wide), lambda i: (i, 0, 0)),
            pl.BlockSpec((1, cells, wide), lambda i: (i, 0, 0)),
            pl.BlockSpec((offsets, fine, wide), lambda i: (0, 0, 0)),
        ],
        out_specs=pl.BlockSpec((1, cells, offsets, fine), lambda i: (i, 0, 0, 0)),
        out_shape=jax.ShapeDtypeStruct((extent, cells, offsets, fine), jnp.bfloat16),
        scratch_shapes=[pltpu.VMEM((fine // 128, offsets * cells, 128), jnp.float32)],
        compiler_params=pltpu.CompilerParams(vmem_limit_bytes=32 * 2**20),
        cost_estimate=pl.CostEstimate(
            flops=2 * extent * cells * wide * offsets * fine,
            transcendentals=0,
            bytes_accessed=extent * cells * (wide * 10 + offsets * fine * 2),
        ),
        name="down_blocks",
    )(mine, theirs, slope, weight)


def planar_moves(swap):
    return [(q, swap(q)) for q in range(8)]


def two_level_body(grad_out, conv_weight, pre_act, down_weight):
    width, extent, plane = grad_out.shape
    taps, _, wide = conv_weight.shape
    block = plane // 4
    k = lax.axis_index("chan")
    q = lax.axis_index(PLANAR)
    far = [(i, i ^ 2) for i in range(4)]
    near = [(i, i ^ 1) for i in range(4)]
    first = planar_moves(lambda d: d ^ (2 if d & 1 == 0 else 4))
    second = planar_moves(lambda d: d ^ (4 if d & 1 == 0 else 2))
    up = [(i, i + 1) for i in range(3)]
    down = [(i + 1, i) for i in range(3)]
    other = [(0, 1), (1, 0)]

    table = conv_weight.reshape(taps * width, wide)
    share = taps * width // 8
    piece = lax.dynamic_slice_in_dim(table, q * share, share, 0)
    got = lax.ppermute(piece, "chan", far)
    got_a = lax.ppermute(got, PLANAR, first)
    got_b = lax.ppermute(got, PLANAR, second)
    got_c = lax.ppermute(got_a, PLANAR, second)
    mine = [got, got_a, got_b, got_c]
    far_weights = mine + [lax.ppermute(v, "pair", other) for v in mine]

    cells = jnp.pad(jnp.transpose(grad_out, (1, 2, 0)), ((0, 0), (NZ, NZ), (0, 0)))

    def window(which):
        return lax.dynamic_slice_in_dim(cells, which * block, block + 2 * NZ, 1)[None]

    def margins(part):
        low = lax.ppermute(part[:, extent - 1 :], SLAB, up)
        high = lax.ppermute(part[:, :1], SLAB, down)
        return low, high

    own = jnp.concatenate([window(k ^ 1), window(k)], 0)
    own_low, own_high = margins(own)
    far_one = lax.ppermute(window(k ^ 3), "chan", far)
    far_two = lax.ppermute(window(k ^ 2), "chan", far)
    one_low, one_high = margins(far_one)
    two_low, two_high = margins(far_two)

    slope = gelu_slope(pre_act.astype(jnp.float32))

    where = jnp.reshape(q, (1,)).astype(jnp.int32)
    begun = conv_blocks(where, own, own_low, own_high, [table], None, 0, jnp.float32)
    sent = conv_blocks(
        where, far_one, one_low, one_high, far_weights, begun, 0, jnp.bfloat16
    )
    theirs = lax.ppermute(sent, "chan", near)
    kept = conv_blocks(where, far_two, two_low, two_high, far_weights, begun, 1, jnp.float32)
    shape = (extent, block, wide)
    return down_blocks(kept.reshape(shape), theirs.reshape(shape), slope, down_weight)


def solution(mesh):
    sizes = dict(mesh.shape)
    four = sizes["chan"] == 4 and all(sizes[axis] == 2 for axis in PLANAR)

    def run(grad_out, conv_weight, pre_act, down_weight):
        split = grad_out.shape[0] // sizes["chan"]
        body = two_level_body if four and split == 128 else general_body
        in_specs = (
            P("chan", ("groups", "space", "pair"), None),
            P(None, "chan", None),
            P(("groups", "space", "pair"), "chan", None),
            P(),
        )
        out_specs = P(("groups", "space", "pair"), "chan", None, None)
        return jax.shard_map(
            body, mesh=mesh, in_specs=in_specs, out_specs=out_specs, check_vma=False
        )(grad_out, conv_weight, pre_act, down_weight)

    return run
```

```python
import functools
import math

import jax
import jax.numpy as jnp
from jax import lax
from jax.experimental import pallas as pl
from jax.experimental.pallas import tpu as pltpu
from jax.sharding import PartitionSpec as P

NZ = 8
PLANAR = ("groups", "space", "pair")
SLAB = ("space", "pair")
COST = (4 * 10**9, 4 * 10**9, 8 * 10**9)


def gelu_slope(values):
    return 0.5 * (1.0 + jax.scipy.special.erf(values / math.sqrt(2.0))) + values * jnp.exp(
        -0.5 * values * values
    ) / math.sqrt(2.0 * math.pi)


def with_halo(cells, sides, width):
    for axis, dim in sides:
        count = lax.axis_size(axis)
        ends = count - 1
        head = lax.slice_in_dim(cells, 0, width, axis=dim)
        tail = lax.slice_in_dim(cells, cells.shape[dim] - width, cells.shape[dim], axis=dim)
        cells = jnp.concatenate(
            [
                lax.ppermute(tail, axis, [(i, (i + 1) % count) for i in range(ends)]),
                cells,
                lax.ppermute(head, axis, [((i + 1) % count, i) for i in range(ends)]),
            ],
            axis=dim,
        )
    return cells


def shifted_stack(padded, depth):
    extent = padded.shape[1] - 2
    plane_len = padded.shape[2]
    widened = jnp.pad(padded, ((0, 0), (0, 0), (depth + 1, depth + 1)))
    z_index = jnp.arange(plane_len, dtype=jnp.int32) % depth
    pieces = []
    for step_x in (-1, 0, 1):
        x_rows = widened[:, 1 - step_x : 1 - step_x + extent, :]
        for step_y in (-1, 0, 1):
            for step_z in (-1, 0, 1):
                offset = step_y * depth + step_z
                piece = x_rows[:, :, depth + 1 - offset : depth + 1 - offset + plane_len]
                inside = (z_index - step_z >= 0) & (z_index - step_z < depth)
                pieces.append(jnp.where(inside, piece, jnp.zeros_like(piece)))
    return jnp.stack(pieces)


def general_body(grad_out, conv_weight, pre_act, down_weight):
    padded = with_halo(grad_out, ((SLAB, 1),), 1)
    stacked = shifted_stack(padded, NZ)
    partial_sum = lax.dot_general(
        stacked, conv_weight, (((0, 1), (0, 1)), ((), ())), preferred_element_type=jnp.float32
    )
    owned = lax.psum_scatter(
        partial_sum.astype(jnp.bfloat16), "chan", scatter_dimension=2, tiled=True
    )
    grad_act = lax.all_to_all(owned, "chan", split_axis=1, concat_axis=2, tiled=True)
    values = pre_act.astype(jnp.float32)
    grad_pre = (grad_act.astype(jnp.float32) * gelu_slope(values)).astype(jnp.bfloat16)
    result = lax.dot_general(
        grad_pre, down_weight, (((2,), (2,)), ((), ())), preferred_element_type=jnp.float32
    )
    return result.astype(jnp.bfloat16)


def piece_order(q):
    first = 2 + 2 * (q & 1)
    second = 6 - first
    return [q, q ^ first, q ^ second, q ^ 6, q ^ 1, q ^ 1 ^ second, q ^ 1 ^ first, q ^ 7]


def conv_kernel(where_ref, *refs, sources, added):
    refs = list(refs)
    groups = []
    for pieces in sources:
        groups.append((refs[:3], refs[3 : 3 + pieces]))
        del refs[: 3 + pieces]
    start_ref = refs.pop(0) if added else None
    out_ref, copies = refs[:2]
    tables, sems = refs[2 : 2 + len(sources)], refs[2 + len(sources) :]
    extent, rows, width = groups[0][0][0].shape
    cells = rows - 2 * NZ

    loads = []
    for (_, weights), table, sem in zip(groups, tables, sems):
        if len(weights) == 1:
            loads.append([pltpu.make_async_copy(weights[0], table, sem.at[0])])
            continue
        order = piece_order(where_ref[0])
        mine, base = [], 0
        for n, piece in enumerate(weights):
            share = piece.shape[0]
            row = pl.multiple_of(base + order[n % 8] * share, 16)
            mine.append(
                pltpu.make_async_copy(piece, table.at[pl.ds(row, share), :], sem.at[n])
            )
            if n % 8 == 7:
                base += 8 * share
        loads.append(mine)
    for mine in loads:
        for load in mine:
            load.start()

    depth_at = lax.broadcasted_iota(jnp.int32, (rows, width), 0) % NZ
    total = start_ref[...] if added else None
    for ((main_ref, low_ref, high_ref), _), table, mine in zip(groups, tables, loads):
        for x in range(extent + 2):
            if x == 0:
                plane = low_ref[...]
            elif x == extent + 1:
                plane = high_ref[...]
            else:
                plane = main_ref[x - 1]
            plane = plane.astype(jnp.float32)
            for step_z in (-1, 0, 1):
                if step_z == 1:
                    moved = jnp.where(depth_at >= 1, pltpu.roll(plane, 1, 0), 0.0)
                elif step_z == -1:
                    moved = jnp.where(depth_at < NZ - 1, pltpu.roll(plane, rows - 1, 0), 0.0)
                else:
                    moved = plane
                for step_y in (-1, 0, 1):
                    at = NZ * (1 - step_y)
                    lane = (3 * (step_y + 1) + step_z + 1) * width
                    copies[x, :, lane : lane + width] = moved[at : at + cells].astype(
                        jnp.bfloat16
                    )
        for load in mine:
            load.wait()
        for step_x in (-1, 0, 1):
            left = copies[1 - step_x : 1 - step_x + extent].reshape(extent * cells, 9 * width)
            right = table[(step_x + 1) * 9 * width : (step_x + 2) * 9 * width]
            term = jnp.dot(left, right, preferred_element_type=jnp.float32)
            total = term if total is None else total + term
    out_ref[...] = total.astype(out_ref.dtype)


def conv_blocks(where, sources, start, kind, flops):
    extent, rows, width = sources[0][0].shape
    wide = sources[0][3][0].shape[1]
    taps = 27
    cells = extent * (rows - 2 * NZ)
    in_specs = [pl.BlockSpec(memory_space=pltpu.SMEM)]
    operands = [where]
    for main, low, high, weights in sources:
        in_specs += [pl.BlockSpec(memory_space=pltpu.VMEM)] * 3
        in_specs += [pl.BlockSpec(memory_space=pl.ANY)] * len(weights)
        operands += [main, low, high, *weights]
    if start is not None:
        in_specs.append(pl.BlockSpec(memory_space=pltpu.VMEM))
        operands.append(start)
    return pl.pallas_call(
        functools.partial(
            conv_kernel, sources=[len(v[3]) for v in sources], added=start is not None
        ),
        in_specs=in_specs,
        out_specs=pl.BlockSpec(memory_space=pltpu.VMEM),
        out_shape=jax.ShapeDtypeStruct((cells, wide), kind),
        scratch_shapes=[pltpu.VMEM((extent + 2, rows - 2 * NZ, 9 * width), jnp.bfloat16)]
        + [pltpu.VMEM((taps * width, wide), jnp.bfloat16)] * len(sources)
        + [pltpu.SemaphoreType.DMA((len(v[3]),)) for v in sources],
        compiler_params=pltpu.CompilerParams(vmem_limit_bytes=28 * 2**20),
        cost_estimate=pl.CostEstimate(flops=flops, transcendentals=0, bytes_accessed=flops // 400),
        name="conv_blocks",
    )(*operands)


def down_kernel(mine_ref, theirs_ref, slope_ref, weight_ref, out_ref):
    act = (mine_ref[0] + theirs_ref[0].astype(jnp.float32)).astype(jnp.bfloat16)
    pre = (act.astype(jnp.float32) * slope_ref[0]).astype(jnp.bfloat16)
    grown = [
        lax.dot_general(
            pre,
            weight_ref[e],
            (((1,), (1,)), ((), ())),
            preferred_element_type=jnp.float32,
        ).astype(out_ref.dtype)
        for e in range(weight_ref.shape[0])
    ]
    out_ref[0] = jnp.swapaxes(jnp.stack(grown), 0, 1)


def down_blocks(mine, theirs, slope, weight):
    extent, cells, wide = slope.shape
    offsets, fine, _ = weight.shape
    return pl.pallas_call(
        down_kernel,
        grid=(extent,),
        in_specs=[
            pl.BlockSpec((1, cells, wide), lambda i: (i, 0, 0)),
            pl.BlockSpec((1, cells, wide), lambda i: (i, 0, 0)),
            pl.BlockSpec((1, cells, wide), lambda i: (i, 0, 0)),
            pl.BlockSpec((offsets, fine, wide), lambda i: (0, 0, 0)),
        ],
        out_specs=pl.BlockSpec((1, cells, offsets, fine), lambda i: (i, 0, 0, 0)),
        out_shape=jax.ShapeDtypeStruct((extent, cells, offsets, fine), jnp.bfloat16),
        compiler_params=pltpu.CompilerParams(vmem_limit_bytes=20 * 2**20),
        name="down_blocks",
    )(mine, theirs, slope, weight)


def planar_moves(swap):
    return [(q, swap(q)) for q in range(8)]


def two_level_body(grad_out, conv_weight, pre_act, down_weight):
    width, extent, plane = grad_out.shape
    taps, _, wide = conv_weight.shape
    block = plane // 4
    k = lax.axis_index("chan")
    q = lax.axis_index(PLANAR)
    far = [(i, i ^ 2) for i in range(4)]
    near = [(i, i ^ 1) for i in range(4)]
    first = planar_moves(lambda d: d ^ (2 if d & 1 == 0 else 4))
    second = planar_moves(lambda d: d ^ (4 if d & 1 == 0 else 2))
    up = [(i, i + 1) for i in range(3)]
    down = [(i + 1, i) for i in range(3)]
    other = [(0, 1), (1, 0)]

    def after(value, *others):
        return lax.optimization_barrier((value, *others))[0]

    def margins(part):
        low = lax.ppermute(part[:, extent - 1 :], SLAB, up)
        high = lax.ppermute(part[:, :1], SLAB, down)
        return low, high

    table = conv_weight.reshape(taps * width, wide)
    share = taps * width // 8
    piece = lax.dynamic_slice_in_dim(table, q * share, share, 0)
    got = lax.ppermute(piece, "chan", far)

    cells = jnp.pad(
        jnp.transpose(after(grad_out, piece), (1, 2, 0)), ((0, 0), (NZ, NZ), (0, 0))
    )

    def window(which):
        return lax.dynamic_slice_in_dim(cells, which * block, block + 2 * NZ, 1)

    where = jnp.reshape(q, (1,)).astype(jnp.int32)
    own_one, own_two = window(k ^ 1), window(k)
    own_low, own_high = margins(jnp.stack([own_one, own_two]))
    begun = conv_blocks(
        where, [(own_one, own_low[0, 0], own_high[0, 0], [table])], None, jnp.float32, COST[0]
    )
    slope = gelu_slope(after(pre_act, piece).astype(jnp.float32))
    got, window_one, window_two = lax.optimization_barrier(
        (got, window(k ^ 3), window(k ^ 2), begun, slope)
    )[:3]
    far_one = lax.ppermute(window_one, "chan", far)
    got_a = lax.ppermute(got, PLANAR, first)
    got_b = lax.ppermute(got, PLANAR, second)
    got_c = lax.ppermute(got_a, PLANAR, second)
    got_b = after(got_b, far_one)
    one_low, one_high = margins(far_one[None])
    far_two = lax.ppermute(after(window_two, far_one), "chan", far)
    got_c, one_low, one_high = lax.optimization_barrier((got_c, one_low, one_high))
    mine = [got, got_a, got_b, got_c]
    pieces = mine + [lax.ppermute(v, "pair", other) for v in mine]

    sent = conv_blocks(
        where,
        [(far_one, one_low[0, 0], one_high[0, 0], pieces)],
        begun,
        jnp.bfloat16,
        COST[1],
    )
    theirs = lax.ppermute(sent, "chan", near)
    far_two = after(far_two, sent)
    two_low, two_high = margins(far_two[None])
    kept = conv_blocks(
        where,
        [
            (own_two, own_low[1, 0], own_high[1, 0], [table]),
            (far_two, two_low[0, 0], two_high[0, 0], pieces),
        ],
        None,
        jnp.float32,
        COST[2],
    )
    shape = (extent, block, wide)
    return down_blocks(kept.reshape(shape), theirs.reshape(shape), slope, down_weight)


def solution(mesh):
    sizes = dict(mesh.shape)
    four = sizes["chan"] == 4 and all(sizes[axis] == 2 for axis in PLANAR)

    def run(grad_out, conv_weight, pre_act, down_weight):
        split = grad_out.shape[0] // sizes["chan"]
        body = two_level_body if four and split == 128 else general_body
        in_specs = (
            P("chan", ("groups", "space", "pair"), None),
            P(None, "chan", None),
            P(("groups", "space", "pair"), "chan", None),
            P(),
        )
        out_specs = P(("groups", "space", "pair"), "chan", None, None)
        return jax.shard_map(
            body, mesh=mesh, in_specs=in_specs, out_specs=out_specs, check_vma=False
        )(grad_out, conv_weight, pre_act, down_weight)

    return run
```

```python
import functools
import math

import jax
import jax.numpy as jnp
from jax import lax
from jax.experimental import pallas as pl
from jax.experimental.pallas import tpu as pltpu
from jax.sharding import PartitionSpec as P

NZ = 8
PLANAR = ("groups", "space", "pair")
SLAB = ("space", "pair")
LIMIT = 20
PART = (1, 1, 1, 4)


def gelu_slope(values):
    return 0.5 * (1.0 + jax.scipy.special.erf(values / math.sqrt(2.0))) + values * jnp.exp(
        -0.5 * values * values
    ) / math.sqrt(2.0 * math.pi)


def with_halo(cells, sides, width):
    for axis, dim in sides:
        count = lax.axis_size(axis)
        ends = count - 1
        head = lax.slice_in_dim(cells, 0, width, axis=dim)
        tail = lax.slice_in_dim(cells, cells.shape[dim] - width, cells.shape[dim], axis=dim)
        cells = jnp.concatenate(
            [
                lax.ppermute(tail, axis, [(i, (i + 1) % count) for i in range(ends)]),
                cells,
                lax.ppermute(head, axis, [((i + 1) % count, i) for i in range(ends)]),
            ],
            axis=dim,
        )
    return cells


def shifted_stack(padded, depth):
    extent = padded.shape[1] - 2
    plane_len = padded.shape[2]
    widened = jnp.pad(padded, ((0, 0), (0, 0), (depth + 1, depth + 1)))
    z_index = jnp.arange(plane_len, dtype=jnp.int32) % depth
    pieces = []
    for step_x in (-1, 0, 1):
        x_rows = widened[:, 1 - step_x : 1 - step_x + extent, :]
        for step_y in (-1, 0, 1):
            for step_z in (-1, 0, 1):
                offset = step_y * depth + step_z
                piece = x_rows[:, :, depth + 1 - offset : depth + 1 - offset + plane_len]
                inside = (z_index - step_z >= 0) & (z_index - step_z < depth)
                pieces.append(jnp.where(inside, piece, jnp.zeros_like(piece)))
    return jnp.stack(pieces)


def general_body(grad_out, conv_weight, pre_act, down_weight):
    padded = with_halo(grad_out, ((SLAB, 1),), 1)
    stacked = shifted_stack(padded, NZ)
    partial_sum = lax.dot_general(
        stacked, conv_weight, (((0, 1), (0, 1)), ((), ())), preferred_element_type=jnp.float32
    )
    owned = lax.psum_scatter(
        partial_sum.astype(jnp.bfloat16), "chan", scatter_dimension=2, tiled=True
    )
    grad_act = lax.all_to_all(owned, "chan", split_axis=1, concat_axis=2, tiled=True)
    values = pre_act.astype(jnp.float32)
    grad_pre = (grad_act.astype(jnp.float32) * gelu_slope(values)).astype(jnp.bfloat16)
    result = lax.dot_general(
        grad_pre, down_weight, (((2,), (2,)), ((), ())), preferred_element_type=jnp.float32
    )
    return result.astype(jnp.bfloat16)


def piece_order(q):
    first = 2 + 2 * (q & 1)
    second = 6 - first
    return [q, q ^ first, q ^ second, q ^ 6, q ^ 1, q ^ 1 ^ second, q ^ 1 ^ first, q ^ 7]


def conv_kernel(where_ref, *refs, sources, added, planes):
    refs = list(refs)
    groups = []
    for margins, pieces in sources:
        cells_refs = refs[: 3 if margins else 1]
        del refs[: len(cells_refs)]
        groups.append((cells_refs, refs[:pieces]))
        del refs[:pieces]
    start_ref = refs.pop(0) if added else None
    out_ref = refs.pop(0)
    for n, (cells_refs, weights) in enumerate(groups):
        if len(weights) == 1:
            groups[n] = (cells_refs, weights[0])
            continue
        table = refs.pop(0)
        for piece, spot in zip(weights, piece_order(where_ref[0])):
            share = piece.shape[0]
            table[pl.ds(pl.multiple_of(spot * share, 16), share), :] = piece[...]
        groups[n] = (cells_refs, table)
    copies = refs.pop(0)

    extent, rows, width = groups[0][0][0].shape
    cells = rows - 2 * NZ
    needed = sorted({plane + step for plane in planes for step in range(3)})
    depth_at = lax.broadcasted_iota(jnp.int32, (rows, width), 0) % NZ
    inner_first = (where_ref[0] & 1) == 0
    totals = [start_ref[plane] if added else None for plane in planes]
    for cells_refs, table in groups:
        for x in needed:
            if x == 0:
                plane = jnp.where(inner_first, cells_refs[2][...], cells_refs[1][...])
            elif x == extent + 1:
                plane = jnp.where(inner_first, cells_refs[1][...], cells_refs[2][...])
            else:
                plane = cells_refs[0][x - 1]
            plane = plane.astype(jnp.float32)
            for step_z in (-1, 0, 1):
                if step_z == 1:
                    moved = jnp.where(depth_at >= 1, pltpu.roll(plane, 1, 0), 0.0)
                elif step_z == -1:
                    moved = jnp.where(depth_at < NZ - 1, pltpu.roll(plane, rows - 1, 0), 0.0)
                else:
                    moved = plane
                for step_y in (-1, 0, 1):
                    at = NZ * (1 - step_y)
                    lane = (3 * (step_y + 1) + step_z + 1) * width
                    copies[needed.index(x), :, lane : lane + width] = moved[
                        at : at + cells
                    ].astype(jnp.bfloat16)
        for step_x in (-1, 0, 1):
            left = jnp.concatenate(
                [copies[needed.index(plane + 1 - step_x)] for plane in planes], axis=0
            )
            right = table[(step_x + 1) * 9 * width : (step_x + 2) * 9 * width]
            term = jnp.dot(left, right, preferred_element_type=jnp.float32)
            for n in range(len(planes)):
                part = term[n * cells : (n + 1) * cells]
                totals[n] = part if totals[n] is None else totals[n] + part
    for n in range(len(planes)):
        out_ref[n] = totals[n].astype(out_ref.dtype)


def conv_blocks(where, sources, start, planes, kind, part=1):
    extent, rows, width = sources[0][0][0].shape
    wide = sources[0][1][0].shape[1]
    table_rows = sum(v.shape[0] for v in sources[0][1])
    cells = rows - 2 * NZ
    needed = len({plane + step for plane in planes for step in range(3)})
    pieces = max(len(v[1]) for v in sources)
    in_specs = [pl.BlockSpec(memory_space=pltpu.SMEM)]
    operands = [where]
    on_chip = pl.BlockSpec(memory_space=pltpu.VMEM)
    for cells_and_margins, weights in sources:
        in_specs += [on_chip] * (len(cells_and_margins) + len(weights))
        operands += [*cells_and_margins, *weights]
    if start is not None:
        in_specs.append(on_chip)
        operands.append(start)
    shape = (len(planes), cells, wide)
    out_shape = [jax.ShapeDtypeStruct(shape, kind)]
    scratch = [pltpu.VMEM((needed, cells, 9 * width), jnp.bfloat16)]
    if pieces > 1:
        out_shape.append(jax.ShapeDtypeStruct((table_rows, wide), jnp.bfloat16))
    return pl.pallas_call(
        functools.partial(
            conv_kernel,
            sources=[(len(v[0]) > 1, len(v[1])) for v in sources],
            added=start is not None,
            planes=planes,
        ),
        in_specs=in_specs,
        out_specs=[on_chip] * len(out_shape),
        out_shape=out_shape,
        scratch_shapes=scratch,
        compiler_params=pltpu.CompilerParams(vmem_limit_bytes=LIMIT * 2**20),
        cost_estimate=pl.CostEstimate(
            flops=2 * math.prod(shape) * table_rows * len(sources) // part,
            transcendentals=0,
            bytes_accessed=(2 * math.prod(shape) + 2 * table_rows * wide * len(sources)) // part,
        ),
        name="conv_blocks",
    )(*operands)


def down_kernel(mine_ref, theirs_ref, slope_ref, weight_ref, *refs):
    out_ref = refs[-1]
    act = (mine_ref[0] + theirs_ref[0].astype(jnp.float32)).astype(jnp.bfloat16)
    pre = (act.astype(jnp.float32) * slope_ref[0]).astype(jnp.bfloat16)
    grown = [
        lax.dot_general(
            pre,
            weight_ref[e],
            (((1,), (1,)), ((), ())),
            preferred_element_type=jnp.float32,
        ).astype(out_ref.dtype)
        for e in range(weight_ref.shape[0])
    ]
    out_ref[0] = jnp.swapaxes(jnp.stack(grown), 0, 1)


def down_blocks(mine, theirs, slope, weight, planes, partly):
    extent, cells, wide = slope.shape
    offsets, fine, _ = weight.shape
    first, step = planes[0], planes[1] - planes[0]
    own_plane = pl.BlockSpec((1, cells, wide), lambda i: (first + step * i, 0, 0))
    in_specs = [
        own_plane,
        pl.BlockSpec((1, cells, wide), lambda i: (i, 0, 0)),
        own_plane,
        pl.BlockSpec((offsets, fine, wide), lambda i: (0, 0, 0)),
    ]
    operands = [mine, theirs, slope, weight]
    if partly is not None:
        in_specs.append(pl.BlockSpec(memory_space=pl.ANY))
        operands.append(partly)
    return pl.pallas_call(
        down_kernel,
        grid=(len(planes),),
        in_specs=in_specs,
        out_specs=pl.BlockSpec(
            (1, cells, offsets, fine), lambda i: (first + step * i, 0, 0, 0)
        ),
        out_shape=jax.ShapeDtypeStruct((extent, cells, offsets, fine), jnp.bfloat16),
        input_output_aliases={} if partly is None else {4: 0},
        compiler_params=pltpu.CompilerParams(vmem_limit_bytes=20 * 2**20),
        cost_estimate=pl.CostEstimate(
            flops=2 * len(planes) * cells * wide * offsets * fine,
            transcendentals=0,
            bytes_accessed=len(planes) * cells * (wide * 10 + offsets * fine * 2),
        ),
        name="down_blocks",
    )(*operands)


def planar_moves(swap):
    return [(q, swap(q)) for q in range(8)]


def two_level_body(grad_out, conv_weight, pre_act, down_weight):
    width, extent, plane = grad_out.shape
    taps, _, wide = conv_weight.shape
    block = plane // 4
    k = lax.axis_index("chan")
    q = lax.axis_index(PLANAR)
    far = [(i, i ^ 2) for i in range(4)]
    near = [(i, i ^ 1) for i in range(4)]
    first = planar_moves(lambda d: d ^ (2 if d & 1 == 0 else 4))
    second = planar_moves(lambda d: d ^ (4 if d & 1 == 0 else 2))
    other = [(0, 1), (1, 0)]
    middle = [(1, 2), (2, 1)]

    def after(value, *others):
        return lax.optimization_barrier((value, *others))[0]

    def margins(part):
        head, tail = part[:, :1], part[:, extent - 1 :]
        inner = lax.ppermute(
            jnp.where(lax.axis_index("pair") == 0, tail, head), "pair", other
        )
        outer = lax.ppermute(
            jnp.where(lax.axis_index("space") == 0, tail, head), SLAB, middle
        )
        return inner, outer

    table = conv_weight.reshape(taps * width, wide)
    share = taps * width // 8
    piece = lax.dynamic_slice_in_dim(table, q * share, share, 0)
    got = lax.ppermute(piece, "chan", far)

    cells = jnp.pad(
        jnp.transpose(after(grad_out, piece), (1, 2, 0)), ((0, 0), (NZ, NZ), (0, 0))
    )

    def window(which):
        return lax.dynamic_slice_in_dim(cells, which * block, block + 2 * NZ, 1)

    where = jnp.reshape(q, (1,)).astype(jnp.int32)
    own_one, own_two = window(k ^ 1), window(k)
    own_inner, own_outer = margins(jnp.stack([own_one, own_two]))
    every, inside, edges = (0, 1, 2, 3), (1, 2), (0, 3)
    begun = conv_blocks(
        where,
        [((own_one, own_inner[0, 0], own_outer[0, 0]), [table])],
        None,
        every,
        jnp.float32,
        PART[0],
    )[0]
    slope = gelu_slope(after(pre_act, piece).astype(jnp.float32))
    got, window_one, window_two = lax.optimization_barrier(
        (got, window(k ^ 3), window(k ^ 2), begun, slope)
    )[:3]
    far_one = lax.ppermute(window_one, "chan", far)
    got_a = lax.ppermute(got, PLANAR, first)
    got_b = lax.ppermute(got, PLANAR, second)
    got_c = lax.ppermute(got_a, PLANAR, second)
    pair_got, pair_a = [lax.ppermute(v, "pair", other) for v in (got, got_a)]
    got_b = after(got_b, far_one)
    pair_b = lax.ppermute(got_b, "pair", other)
    far_two = lax.ppermute(after(window_two, far_one), "chan", far)
    one_inner, one_outer = margins(far_one[None])
    got_c, pair_got, pair_a, one_inner, one_outer = lax.optimization_barrier(
        (got_c, pair_got, pair_a, one_inner, one_outer)
    )
    pair_c = lax.ppermute(got_c, "pair", other)
    pieces = [got, got_a, got_b, got_c, pair_got, pair_a, pair_b, pair_c]

    sent_inside, far_table = conv_blocks(
        where, [((far_one,), pieces)], begun, inside, jnp.bfloat16, PART[1]
    )
    theirs_inside = lax.ppermute(sent_inside, "chan", near)
    far_one = after(far_one, sent_inside)
    sent_edges = conv_blocks(
        where,
        [((far_one, one_inner[0, 0], one_outer[0, 0]), [far_table])],
        begun,
        edges,
        jnp.bfloat16,
        PART[2],
    )[0]
    theirs_edges = lax.ppermute(sent_edges, "chan", near)
    far_two = after(far_two, sent_edges)
    two_inner, two_outer = margins(far_two[None])
    kept = conv_blocks(
        where,
        [
            ((own_two, own_inner[1, 0], own_outer[1, 0]), [table]),
            ((far_two, two_inner[0, 0], two_outer[0, 0]), [far_table]),
        ],
        None,
        every,
        jnp.float32,
        PART[3],
    )[0]
    partly = down_blocks(kept, theirs_inside, slope, down_weight, inside, None)
    return down_blocks(kept, theirs_edges, slope, down_weight, edges, partly)


def solution(mesh):
    sizes = dict(mesh.shape)
    four = sizes["chan"] == 4 and all(sizes[axis] == 2 for axis in PLANAR)

    def run(grad_out, conv_weight, pre_act, down_weight):
        split = grad_out.shape[0] // sizes["chan"]
        body = two_level_body if four and split == 128 and grad_out.shape[1] == 32 else general_body
        in_specs = (
            P("chan", ("groups", "space", "pair"), None),
            P(None, "chan", None),
            P(("groups", "space", "pair"), "chan", None),
            P(),
        )
        out_specs = P(("groups", "space", "pair"), "chan", None, None)
        return jax.shard_map(
            body, mesh=mesh, in_specs=in_specs, out_specs=out_specs, check_vma=False
        )(grad_out, conv_weight, pre_act, down_weight)

    return run
```

```python
import functools
import math

import jax
import jax.numpy as jnp
from jax import lax
from jax.experimental import pallas as pl
from jax.experimental.pallas import tpu as pltpu
from jax.sharding import PartitionSpec as P

NZ = 8
PLANAR = ("groups", "space", "pair")
SLAB = ("space", "pair")
LIMIT = 20
PART = (1, 1, 1, 2)
GROUPS = ((1,), (2, 0), (3,))


def gelu_slope(values):
    return 0.5 * (1.0 + jax.scipy.special.erf(values / math.sqrt(2.0))) + values * jnp.exp(
        -0.5 * values * values
    ) / math.sqrt(2.0 * math.pi)


def with_halo(cells, sides, width):
    for axis, dim in sides:
        count = lax.axis_size(axis)
        ends = count - 1
        head = lax.slice_in_dim(cells, 0, width, axis=dim)
        tail = lax.slice_in_dim(cells, cells.shape[dim] - width, cells.shape[dim], axis=dim)
        cells = jnp.concatenate(
            [
                lax.ppermute(tail, axis, [(i, (i + 1) % count) for i in range(ends)]),
                cells,
                lax.ppermute(head, axis, [((i + 1) % count, i) for i in range(ends)]),
            ],
            axis=dim,
        )
    return cells


def shifted_stack(padded, depth):
    extent = padded.shape[1] - 2
    plane_len = padded.shape[2]
    widened = jnp.pad(padded, ((0, 0), (0, 0), (depth + 1, depth + 1)))
    z_index = jnp.arange(plane_len, dtype=jnp.int32) % depth
    pieces = []
    for step_x in (-1, 0, 1):
        x_rows = widened[:, 1 - step_x : 1 - step_x + extent, :]
        for step_y in (-1, 0, 1):
            for step_z in (-1, 0, 1):
                offset = step_y * depth + step_z
                piece = x_rows[:, :, depth + 1 - offset : depth + 1 - offset + plane_len]
                inside = (z_index - step_z >= 0) & (z_index - step_z < depth)
                pieces.append(jnp.where(inside, piece, jnp.zeros_like(piece)))
    return jnp.stack(pieces)


def general_body(grad_out, conv_weight, pre_act, down_weight):
    padded = with_halo(grad_out, ((SLAB, 1),), 1)
    stacked = shifted_stack(padded, NZ)
    partial_sum = lax.dot_general(
        stacked, conv_weight, (((0, 1), (0, 1)), ((), ())), preferred_element_type=jnp.float32
    )
    owned = lax.psum_scatter(
        partial_sum.astype(jnp.bfloat16), "chan", scatter_dimension=2, tiled=True
    )
    grad_act = lax.all_to_all(owned, "chan", split_axis=1, concat_axis=2, tiled=True)
    values = pre_act.astype(jnp.float32)
    grad_pre = (grad_act.astype(jnp.float32) * gelu_slope(values)).astype(jnp.bfloat16)
    result = lax.dot_general(
        grad_pre, down_weight, (((2,), (2,)), ((), ())), preferred_element_type=jnp.float32
    )
    return result.astype(jnp.bfloat16)


def piece_order(q):
    first = 2 + 2 * (q & 1)
    second = 6 - first
    return [q, q ^ first, q ^ second, q ^ 6, q ^ 1, q ^ 1 ^ second, q ^ 1 ^ first, q ^ 7]


def conv_kernel(where_ref, *refs, sources, added, planes):
    refs = list(refs)
    groups = []
    for margins, pieces in sources:
        cells_refs = refs[: 3 if margins else 1]
        del refs[: len(cells_refs)]
        groups.append((cells_refs, refs[:pieces]))
        del refs[:pieces]
    start_ref = refs.pop(0) if added else None
    out_ref = refs.pop(0)
    for n, (cells_refs, weights) in enumerate(groups):
        if len(weights) == 1:
            groups[n] = (cells_refs, weights[0])
            continue
        table = refs.pop(0)
        for piece, spot in zip(weights, piece_order(where_ref[0])):
            share = piece.shape[0]
            table[pl.ds(pl.multiple_of(spot * share, 16), share), :] = piece[...]
        groups[n] = (cells_refs, table)
    copies = refs.pop(0)

    extent, rows, width = groups[0][0][0].shape
    cells = rows - 2 * NZ
    needed = sorted({plane + step for plane in planes for step in range(3)})
    depth_at = lax.broadcasted_iota(jnp.int32, (rows, width), 0) % NZ
    inner_first = (where_ref[0] & 1) == 0
    totals = [start_ref[plane] if added else None for plane in planes]
    for cells_refs, table in groups:
        for x in needed:
            if x == 0:
                plane = jnp.where(inner_first, cells_refs[2][...], cells_refs[1][...])
            elif x == extent + 1:
                plane = jnp.where(inner_first, cells_refs[1][...], cells_refs[2][...])
            else:
                plane = cells_refs[0][x - 1]
            plane = plane.astype(jnp.float32)
            for step_z in (-1, 0, 1):
                if step_z == 1:
                    moved = jnp.where(depth_at >= 1, pltpu.roll(plane, 1, 0), 0.0)
                elif step_z == -1:
                    moved = jnp.where(depth_at < NZ - 1, pltpu.roll(plane, rows - 1, 0), 0.0)
                else:
                    moved = plane
                for step_y in (-1, 0, 1):
                    at = NZ * (1 - step_y)
                    lane = (3 * (step_y + 1) + step_z + 1) * width
                    copies[needed.index(x), :, lane : lane + width] = moved[
                        at : at + cells
                    ].astype(jnp.bfloat16)
        for step_x in (-1, 0, 1):
            left = jnp.concatenate(
                [copies[needed.index(plane + 1 - step_x)] for plane in planes], axis=0
            )
            right = table[(step_x + 1) * 9 * width : (step_x + 2) * 9 * width]
            term = jnp.dot(left, right, preferred_element_type=jnp.float32)
            for n in range(len(planes)):
                part = term[n * cells : (n + 1) * cells]
                totals[n] = part if totals[n] is None else totals[n] + part
    for n in range(len(planes)):
        out_ref[n] = totals[n].astype(out_ref.dtype)


def conv_blocks(where, sources, start, planes, kind, part=1):
    extent, rows, width = sources[0][0][0].shape
    wide = sources[0][1][0].shape[1]
    table_rows = sum(v.shape[0] for v in sources[0][1])
    cells = rows - 2 * NZ
    needed = len({plane + step for plane in planes for step in range(3)})
    pieces = max(len(v[1]) for v in sources)
    in_specs = [pl.BlockSpec(memory_space=pltpu.SMEM)]
    operands = [where]
    on_chip = pl.BlockSpec(memory_space=pltpu.VMEM)
    for cells_and_margins, weights in sources:
        in_specs += [on_chip] * (len(cells_and_margins) + len(weights))
        operands += [*cells_and_margins, *weights]
    if start is not None:
        in_specs.append(on_chip)
        operands.append(start)
    shape = (len(planes), cells, wide)
    out_shape = [jax.ShapeDtypeStruct(shape, kind)]
    scratch = [pltpu.VMEM((needed, cells, 9 * width), jnp.bfloat16)]
    if pieces > 1:
        out_shape.append(jax.ShapeDtypeStruct((table_rows, wide), jnp.bfloat16))
    return pl.pallas_call(
        functools.partial(
            conv_kernel,
            sources=[(len(v[0]) > 1, len(v[1])) for v in sources],
            added=start is not None,
            planes=planes,
        ),
        in_specs=in_specs,
        out_specs=[on_chip] * len(out_shape),
        out_shape=out_shape,
        scratch_shapes=scratch,
        compiler_params=pltpu.CompilerParams(vmem_limit_bytes=LIMIT * 2**20),
        cost_estimate=pl.CostEstimate(
            flops=2 * math.prod(shape) * table_rows * len(sources) // part,
            transcendentals=0,
            bytes_accessed=(2 * math.prod(shape) + 2 * table_rows * wide * len(sources)) // part,
        ),
        name="conv_blocks",
    )(*operands)


def down_kernel(mine_ref, theirs_ref, slope_ref, weight_ref, *refs, first, step):
    out_ref = refs[-1]
    at = pl.program_id(0)
    plane = first + step * at
    act = (mine_ref[plane] + theirs_ref[at].astype(jnp.float32)).astype(jnp.bfloat16)
    pre = (act.astype(jnp.float32) * slope_ref[plane]).astype(jnp.bfloat16)
    grown = [
        lax.dot_general(
            pre,
            weight_ref[e],
            (((1,), (1,)), ((), ())),
            preferred_element_type=jnp.float32,
        ).astype(out_ref.dtype)
        for e in range(weight_ref.shape[0])
    ]
    out_ref[0] = jnp.swapaxes(jnp.stack(grown), 0, 1)


def down_blocks(mine, theirs, slope, weight, planes, partly):
    extent, cells, wide = slope.shape
    offsets, fine, _ = weight.shape
    first = planes[0]
    step = planes[1] - first if len(planes) > 1 else 0
    on_chip = pl.BlockSpec(memory_space=pltpu.VMEM)
    in_specs = [on_chip] * 4
    operands = [mine, theirs, slope, weight]
    if partly is not None:
        in_specs.append(pl.BlockSpec(memory_space=pl.ANY))
        operands.append(partly)
    return pl.pallas_call(
        functools.partial(down_kernel, first=first, step=step),
        grid=(len(planes),),
        in_specs=in_specs,
        out_specs=pl.BlockSpec(
            (1, cells, offsets, fine), lambda i: (first + step * i, 0, 0, 0)
        ),
        out_shape=jax.ShapeDtypeStruct((extent, cells, offsets, fine), jnp.bfloat16),
        input_output_aliases={} if partly is None else {4: 0},
        compiler_params=pltpu.CompilerParams(vmem_limit_bytes=20 * 2**20),
        cost_estimate=pl.CostEstimate(
            flops=2 * len(planes) * cells * wide * offsets * fine,
            transcendentals=0,
            bytes_accessed=len(planes) * cells * (wide * 10 + offsets * fine * 2),
        ),
        name="down_blocks",
    )(*operands)


def planar_moves(swap):
    return [(q, swap(q)) for q in range(8)]


def two_level_body(grad_out, conv_weight, pre_act, down_weight):
    width, extent, plane = grad_out.shape
    taps, _, wide = conv_weight.shape
    block = plane // 4
    k = lax.axis_index("chan")
    q = lax.axis_index(PLANAR)
    far = [(i, i ^ 2) for i in range(4)]
    near = [(i, i ^ 1) for i in range(4)]
    first = planar_moves(lambda d: d ^ (2 if d & 1 == 0 else 4))
    second = planar_moves(lambda d: d ^ (4 if d & 1 == 0 else 2))
    other = [(0, 1), (1, 0)]
    middle = [(1, 2), (2, 1)]

    def after(value, *others):
        return lax.optimization_barrier((value, *others))[0]

    def margins(part):
        head, tail = part[:, :1], part[:, extent - 1 :]
        inner = lax.ppermute(
            jnp.where(lax.axis_index("pair") == 0, tail, head), "pair", other
        )
        outer = lax.ppermute(
            jnp.where(lax.axis_index("space") == 0, tail, head), SLAB, middle
        )
        return inner, outer

    table = conv_weight.reshape(taps * width, wide)
    share = taps * width // 8
    piece = lax.dynamic_slice_in_dim(table, q * share, share, 0)
    got = lax.ppermute(piece, "chan", far)

    cells = jnp.pad(
        jnp.transpose(after(grad_out, piece), (1, 2, 0)), ((0, 0), (NZ, NZ), (0, 0))
    )

    def window(which):
        return lax.dynamic_slice_in_dim(cells, which * block, block + 2 * NZ, 1)

    where = jnp.reshape(q, (1,)).astype(jnp.int32)
    own_one, own_two = window(k ^ 1), window(k)
    own_inner, own_outer = margins(jnp.stack([own_one, own_two]))
    every = (0, 1, 2, 3)
    begun, kept = [
        conv_blocks(
            where,
            [((cells_of, own_inner[n, 0], own_outer[n, 0]), [table])],
            None,
            every,
            jnp.float32,
            PART[0],
        )[0]
        for n, cells_of in enumerate((own_one, own_two))
    ]
    slope = gelu_slope(after(pre_act, piece).astype(jnp.float32))
    got, window_one, window_two = lax.optimization_barrier(
        (got, window(k ^ 3), window(k ^ 2), begun, kept, slope)
    )[:3]
    far_one = lax.ppermute(window_one, "chan", far)
    got_a = lax.ppermute(got, PLANAR, first)
    got_b = lax.ppermute(got, PLANAR, second)
    got_c = lax.ppermute(got_a, PLANAR, second)
    pair_got, pair_a = [lax.ppermute(v, "pair", other) for v in (got, got_a)]
    got_b = after(got_b, far_one)
    pair_b = lax.ppermute(got_b, "pair", other)
    far_two = lax.ppermute(after(window_two, far_one), "chan", far)
    one_inner, one_outer = margins(far_one[None])
    got_c, pair_got, pair_a, one_inner, one_outer = lax.optimization_barrier(
        (got_c, pair_got, pair_a, one_inner, one_outer)
    )
    pair_c = lax.ppermute(got_c, "pair", other)
    pieces = [got, got_a, got_b, got_c, pair_got, pair_a, pair_b, pair_c]

    sent, far_table = conv_blocks(
        where, [((far_one,), pieces)], begun, GROUPS[0], jnp.bfloat16, PART[1]
    )
    theirs = [lax.ppermute(sent, "chan", near)]
    for planes in GROUPS[1:]:
        far_one = after(far_one, sent)
        one = (far_one, one_inner[0, 0], one_outer[0, 0])
        sent = conv_blocks(
            where, [(one, [far_table])], begun, planes, jnp.bfloat16, PART[2]
        )[0]
        theirs.append(lax.ppermute(sent, "chan", near))
    far_two = after(far_two, sent)
    two_inner, two_outer = margins(far_two[None])
    two = (far_two, two_inner[0, 0], two_outer[0, 0])
    kept = conv_blocks(where, [(two, [far_table])], kept, every, jnp.float32, PART[3])[0]
    result = None
    for planes, part in zip(GROUPS, theirs):
        result = down_blocks(kept, part, slope, down_weight, planes, result)
    return result


def solution(mesh):
    sizes = dict(mesh.shape)
    four = sizes["chan"] == 4 and all(sizes[axis] == 2 for axis in PLANAR)

    def run(grad_out, conv_weight, pre_act, down_weight):
        split = grad_out.shape[0] // sizes["chan"]
        body = two_level_body if four and split == 128 and grad_out.shape[1] == 32 else general_body
        in_specs = (
            P("chan", ("groups", "space", "pair"), None),
            P(None, "chan", None),
            P(("groups", "space", "pair"), "chan", None),
            P(),
        )
        out_specs = P(("groups", "space", "pair"), "chan", None, None)
        return jax.shard_map(
            body, mesh=mesh, in_specs=in_specs, out_specs=out_specs, check_vma=False
        )(grad_out, conv_weight, pre_act, down_weight)

    return run
```

```python
import functools
import math

import jax
import jax.numpy as jnp
from jax import lax
from jax.experimental import pallas as pl
from jax.experimental.pallas import tpu as pltpu
from jax.sharding import PartitionSpec as P

NZ = 8
PLANAR = ("groups", "space", "pair")
SLAB = ("space", "pair")
LIMIT = 20
PART = (1, 1, 1, 2)
GROUPS = ((1,), (2, 0), (3,))


def gelu_slope(values):
    return 0.5 * (1.0 + jax.scipy.special.erf(values / math.sqrt(2.0))) + values * jnp.exp(
        -0.5 * values * values
    ) / math.sqrt(2.0 * math.pi)


def with_halo(cells, sides, width):
    for axis, dim in sides:
        count = lax.axis_size(axis)
        ends = count - 1
        head = lax.slice_in_dim(cells, 0, width, axis=dim)
        tail = lax.slice_in_dim(cells, cells.shape[dim] - width, cells.shape[dim], axis=dim)
        cells = jnp.concatenate(
            [
                lax.ppermute(tail, axis, [(i, (i + 1) % count) for i in range(ends)]),
                cells,
                lax.ppermute(head, axis, [((i + 1) % count, i) for i in range(ends)]),
            ],
            axis=dim,
        )
    return cells


def shifted_stack(padded, depth):
    extent = padded.shape[1] - 2
    plane_len = padded.shape[2]
    widened = jnp.pad(padded, ((0, 0), (0, 0), (depth + 1, depth + 1)))
    z_index = jnp.arange(plane_len, dtype=jnp.int32) % depth
    pieces = []
    for step_x in (-1, 0, 1):
        x_rows = widened[:, 1 - step_x : 1 - step_x + extent, :]
        for step_y in (-1, 0, 1):
            for step_z in (-1, 0, 1):
                offset = step_y * depth + step_z
                piece = x_rows[:, :, depth + 1 - offset : depth + 1 - offset + plane_len]
                inside = (z_index - step_z >= 0) & (z_index - step_z < depth)
                pieces.append(jnp.where(inside, piece, jnp.zeros_like(piece)))
    return jnp.stack(pieces)


def general_body(grad_out, conv_weight, pre_act, down_weight):
    padded = with_halo(grad_out, ((SLAB, 1),), 1)
    stacked = shifted_stack(padded, NZ)
    partial_sum = lax.dot_general(
        stacked, conv_weight, (((0, 1), (0, 1)), ((), ())), preferred_element_type=jnp.float32
    )
    owned = lax.psum_scatter(
        partial_sum.astype(jnp.bfloat16), "chan", scatter_dimension=2, tiled=True
    )
    grad_act = lax.all_to_all(owned, "chan", split_axis=1, concat_axis=2, tiled=True)
    values = pre_act.astype(jnp.float32)
    grad_pre = (grad_act.astype(jnp.float32) * gelu_slope(values)).astype(jnp.bfloat16)
    result = lax.dot_general(
        grad_pre, down_weight, (((2,), (2,)), ((), ())), preferred_element_type=jnp.float32
    )
    return result.astype(jnp.bfloat16)


def piece_order(q):
    first = 2 + 2 * (q & 1)
    second = 6 - first
    return [q, q ^ first, q ^ second, q ^ 6, q ^ 1, q ^ 1 ^ second, q ^ 1 ^ first, q ^ 7]


def conv_kernel(where_ref, *refs, sources, added, planes):
    refs = list(refs)
    groups = []
    for margins, pieces in sources:
        cells_refs = refs[: 3 if margins else 1]
        del refs[: len(cells_refs)]
        groups.append((cells_refs, refs[:pieces]))
        del refs[:pieces]
    start_ref = refs.pop(0) if added else None
    out_ref = refs.pop(0)
    for n, (cells_refs, weights) in enumerate(groups):
        if len(weights) == 1:
            groups[n] = (cells_refs, weights[0])
            continue
        table = refs.pop(0)
        for piece, spot in zip(weights, piece_order(where_ref[0])):
            share = piece.shape[0]
            table[pl.ds(pl.multiple_of(spot * share, 16), share), :] = piece[...]
        groups[n] = (cells_refs, table)
    copies = refs.pop(0)

    extent, rows, width = groups[0][0][0].shape
    cells = rows - 2 * NZ
    needed = sorted({plane + step for plane in planes for step in range(3)})
    depth_at = lax.broadcasted_iota(jnp.int32, (rows, width), 0) % NZ
    inner_first = (where_ref[0] & 1) == 0
    totals = [start_ref[plane] if added else None for plane in planes]
    for cells_refs, table in groups:
        for x in needed:
            if x == 0:
                plane = jnp.where(inner_first, cells_refs[2][...], cells_refs[1][...])
            elif x == extent + 1:
                plane = jnp.where(inner_first, cells_refs[1][...], cells_refs[2][...])
            else:
                plane = cells_refs[0][x - 1]
            plane = plane.astype(jnp.float32)
            for step_z in (-1, 0, 1):
                if step_z == 1:
                    moved = jnp.where(depth_at >= 1, pltpu.roll(plane, 1, 0), 0.0)
                elif step_z == -1:
                    moved = jnp.where(depth_at < NZ - 1, pltpu.roll(plane, rows - 1, 0), 0.0)
                else:
                    moved = plane
                for step_y in (-1, 0, 1):
                    at = NZ * (1 - step_y)
                    lane = (3 * (step_y + 1) + step_z + 1) * width
                    copies[needed.index(x), :, lane : lane + width] = moved[
                        at : at + cells
                    ].astype(jnp.bfloat16)
        for step_x in (-1, 0, 1):
            left = jnp.concatenate(
                [copies[needed.index(plane + 1 - step_x)] for plane in planes], axis=0
            )
            right = table[(step_x + 1) * 9 * width : (step_x + 2) * 9 * width]
            term = jnp.dot(left, right, preferred_element_type=jnp.float32)
            for n in range(len(planes)):
                part = term[n * cells : (n + 1) * cells]
                totals[n] = part if totals[n] is None else totals[n] + part
    for n in range(len(planes)):
        out_ref[n] = totals[n].astype(out_ref.dtype)


def conv_blocks(where, sources, start, planes, kind, part=1):
    extent, rows, width = sources[0][0][0].shape
    wide = sources[0][1][0].shape[1]
    table_rows = sum(v.shape[0] for v in sources[0][1])
    cells = rows - 2 * NZ
    needed = len({plane + step for plane in planes for step in range(3)})
    pieces = max(len(v[1]) for v in sources)
    in_specs = [pl.BlockSpec(memory_space=pltpu.SMEM)]
    operands = [where]
    on_chip = pl.BlockSpec(memory_space=pltpu.VMEM)
    for cells_and_margins, weights in sources:
        in_specs += [on_chip] * (len(cells_and_margins) + len(weights))
        operands += [*cells_and_margins, *weights]
    if start is not None:
        in_specs.append(on_chip)
        operands.append(start)
    shape = (len(planes), cells, wide)
    out_shape = [jax.ShapeDtypeStruct(shape, kind)]
    scratch = [pltpu.VMEM((needed, cells, 9 * width), jnp.bfloat16)]
    if pieces > 1:
        out_shape.append(jax.ShapeDtypeStruct((table_rows, wide), jnp.bfloat16))
    return pl.pallas_call(
        functools.partial(
            conv_kernel,
            sources=[(len(v[0]) > 1, len(v[1])) for v in sources],
            added=start is not None,
            planes=planes,
        ),
        in_specs=in_specs,
        out_specs=[on_chip] * len(out_shape),
        out_shape=out_shape,
        scratch_shapes=scratch,
        compiler_params=pltpu.CompilerParams(vmem_limit_bytes=LIMIT * 2**20),
        cost_estimate=pl.CostEstimate(
            flops=2 * math.prod(shape) * table_rows * len(sources) // part,
            transcendentals=0,
            bytes_accessed=(2 * math.prod(shape) + 2 * table_rows * wide * len(sources)) // part,
        ),
        name="conv_blocks",
    )(*operands)


def down_kernel(mine_ref, theirs_ref, slope_ref, weight_ref, *refs, planes):
    out_ref, ready, sems = refs[-3:]
    cells = ready.shape[1]
    step = cells // 4
    copies = []
    for at, plane in enumerate(planes):
        act = (mine_ref[plane] + theirs_ref[at].astype(jnp.float32)).astype(jnp.bfloat16)
        pre = (act.astype(jnp.float32) * slope_ref[plane]).astype(jnp.bfloat16)
        grown = [
            lax.dot_general(
                pre,
                weight_ref[e],
                (((1,), (1,)), ((), ())),
                preferred_element_type=jnp.float32,
            ).astype(out_ref.dtype)
            for e in range(weight_ref.shape[0])
        ]
        for low in range(0, cells, step):
            part = jnp.stack([v[low : low + step] for v in grown])
            ready[at, low : low + step] = jnp.swapaxes(part, 0, 1)
            copies.append(
                pltpu.make_async_copy(
                    ready.at[at, pl.ds(low, step)],
                    out_ref.at[plane, pl.ds(low, step)],
                    sems.at[len(copies)],
                )
            )
            copies[-1].start()
    for copy in copies:
        copy.wait()


def down_blocks(mine, theirs, slope, weight, planes, partly):
    extent, cells, wide = slope.shape
    offsets, fine, _ = weight.shape
    in_specs = [pl.BlockSpec(memory_space=pltpu.VMEM)] * 4
    operands = [mine, theirs, slope, weight]
    if partly is not None:
        in_specs.append(pl.BlockSpec(memory_space=pl.ANY))
        operands.append(partly)
    return pl.pallas_call(
        functools.partial(down_kernel, planes=planes),
        in_specs=in_specs,
        out_specs=pl.BlockSpec(memory_space=pl.ANY),
        out_shape=jax.ShapeDtypeStruct((extent, cells, offsets, fine), jnp.bfloat16),
        scratch_shapes=[
            pltpu.VMEM((len(planes), cells, offsets, fine), jnp.bfloat16),
            pltpu.SemaphoreType.DMA((4 * len(planes),)),
        ],
        input_output_aliases={} if partly is None else {4: 0},
        compiler_params=pltpu.CompilerParams(vmem_limit_bytes=20 * 2**20),
        cost_estimate=pl.CostEstimate(
            flops=2 * len(planes) * cells * wide * offsets * fine,
            transcendentals=0,
            bytes_accessed=len(planes) * cells * (wide * 10 + offsets * fine * 2),
        ),
        name="down_blocks",
    )(*operands)


def planar_moves(swap):
    return [(q, swap(q)) for q in range(8)]


def two_level_body(grad_out, conv_weight, pre_act, down_weight):
    width, extent, plane = grad_out.shape
    taps, _, wide = conv_weight.shape
    block = plane // 4
    k = lax.axis_index("chan")
    q = lax.axis_index(PLANAR)
    far = [(i, i ^ 2) for i in range(4)]
    near = [(i, i ^ 1) for i in range(4)]
    first = planar_moves(lambda d: d ^ (2 if d & 1 == 0 else 4))
    second = planar_moves(lambda d: d ^ (4 if d & 1 == 0 else 2))
    other = [(0, 1), (1, 0)]
    middle = [(1, 2), (2, 1)]

    def after(value, *others):
        return lax.optimization_barrier((value, *others))[0]

    def margins(part):
        head, tail = part[:, :1], part[:, extent - 1 :]
        inner = lax.ppermute(
            jnp.where(lax.axis_index("pair") == 0, tail, head), "pair", other
        )
        outer = lax.ppermute(
            jnp.where(lax.axis_index("space") == 0, tail, head), SLAB, middle
        )
        return inner, outer

    table = conv_weight.reshape(taps * width, wide)
    share = taps * width // 8
    piece = lax.dynamic_slice_in_dim(table, q * share, share, 0)
    got = lax.ppermute(piece, "chan", far)

    cells = jnp.pad(
        jnp.transpose(after(grad_out, piece), (1, 2, 0)), ((0, 0), (NZ, NZ), (0, 0))
    )

    def window(which):
        return lax.dynamic_slice_in_dim(cells, which * block, block + 2 * NZ, 1)

    where = jnp.reshape(q, (1,)).astype(jnp.int32)
    own_one, own_two = window(k ^ 1), window(k)
    own_inner, own_outer = margins(jnp.stack([own_one, own_two]))
    every = (0, 1, 2, 3)
    begun, kept = [
        conv_blocks(
            where,
            [((cells_of, own_inner[n, 0], own_outer[n, 0]), [table])],
            None,
            every,
            jnp.float32,
            PART[0],
        )[0]
        for n, cells_of in enumerate((own_one, own_two))
    ]
    slope = gelu_slope(after(pre_act, piece).astype(jnp.float32))
    got, window_one, window_two = lax.optimization_barrier(
        (got, window(k ^ 3), window(k ^ 2), begun, kept, slope)
    )[:3]
    far_one = lax.ppermute(window_one, "chan", far)
    got_a = lax.ppermute(got, PLANAR, first)
    got_b = lax.ppermute(got, PLANAR, second)
    got_c = lax.ppermute(got_a, PLANAR, second)
    pair_got, pair_a = [lax.ppermute(v, "pair", other) for v in (got, got_a)]
    got_b = after(got_b, far_one)
    pair_b = lax.ppermute(got_b, "pair", other)
    far_two = lax.ppermute(after(window_two, far_one), "chan", far)
    one_inner, one_outer = margins(far_one[None])
    got_c, pair_got, pair_a, one_outer = lax.optimization_barrier(
        (got_c, pair_got, pair_a, one_outer)
    )
    pair_c = lax.ppermute(got_c, "pair", other)
    pieces = [got, got_a, got_b, got_c, pair_got, pair_a, pair_b, pair_c]

    sent, far_table = conv_blocks(
        where, [((far_one,), pieces)], begun, GROUPS[0], jnp.bfloat16, PART[1]
    )
    theirs = [lax.ppermute(sent, "chan", near)]
    for planes in GROUPS[1:]:
        far_one = after(far_one, sent)
        one = (far_one, one_inner[0, 0], one_outer[0, 0])
        sent = conv_blocks(
            where, [(one, [far_table])], begun, planes, jnp.bfloat16, PART[2]
        )[0]
        theirs.append(lax.ppermute(sent, "chan", near))
    far_two = after(far_two, sent)
    two_inner, two_outer = margins(far_two[None])
    two = (far_two, two_inner[0, 0], two_outer[0, 0])
    kept = conv_blocks(where, [(two, [far_table])], kept, every, jnp.float32, PART[3])[0]
    result = None
    for planes, part in zip(GROUPS, theirs):
        result = down_blocks(kept, part, slope, down_weight, planes, result)
    return result


def solution(mesh):
    sizes = dict(mesh.shape)
    four = sizes["chan"] == 4 and all(sizes[axis] == 2 for axis in PLANAR)

    def run(grad_out, conv_weight, pre_act, down_weight):
        split = grad_out.shape[0] // sizes["chan"]
        body = two_level_body if four and split == 128 and grad_out.shape[1] == 32 else general_body
        in_specs = (
            P("chan", ("groups", "space", "pair"), None),
            P(None, "chan", None),
            P(("groups", "space", "pair"), "chan", None),
            P(),
        )
        out_specs = P(("groups", "space", "pair"), "chan", None, None)
        return jax.shard_map(
            body, mesh=mesh, in_specs=in_specs, out_specs=out_specs, check_vma=False
        )(grad_out, conv_weight, pre_act, down_weight)

    return run
```

```python
import functools
import math

import jax
import jax.numpy as jnp
from jax import lax
from jax.experimental import pallas as pl
from jax.experimental.pallas import tpu as pltpu
from jax.sharding import PartitionSpec as P

NZ = 8
PLANAR = ("groups", "space", "pair")
SLAB = ("space", "pair")
LIMIT = 20
PART = (1, 1, 1, 2)
GROUPS = ((1,), (2, 0), (3,))


def gelu_slope(values):
    return 0.5 * (1.0 + jax.scipy.special.erf(values / math.sqrt(2.0))) + values * jnp.exp(
        -0.5 * values * values
    ) / math.sqrt(2.0 * math.pi)


def with_halo(cells, sides, width):
    for axis, dim in sides:
        count = lax.axis_size(axis)
        ends = count - 1
        head = lax.slice_in_dim(cells, 0, width, axis=dim)
        tail = lax.slice_in_dim(cells, cells.shape[dim] - width, cells.shape[dim], axis=dim)
        cells = jnp.concatenate(
            [
                lax.ppermute(tail, axis, [(i, (i + 1) % count) for i in range(ends)]),
                cells,
                lax.ppermute(head, axis, [((i + 1) % count, i) for i in range(ends)]),
            ],
            axis=dim,
        )
    return cells


def shifted_stack(padded, depth):
    extent = padded.shape[1] - 2
    plane_len = padded.shape[2]
    widened = jnp.pad(padded, ((0, 0), (0, 0), (depth + 1, depth + 1)))
    z_index = jnp.arange(plane_len, dtype=jnp.int32) % depth
    pieces = []
    for step_x in (-1, 0, 1):
        x_rows = widened[:, 1 - step_x : 1 - step_x + extent, :]
        for step_y in (-1, 0, 1):
            for step_z in (-1, 0, 1):
                offset = step_y * depth + step_z
                piece = x_rows[:, :, depth + 1 - offset : depth + 1 - offset + plane_len]
                inside = (z_index - step_z >= 0) & (z_index - step_z < depth)
                pieces.append(jnp.where(inside, piece, jnp.zeros_like(piece)))
    return jnp.stack(pieces)


def general_body(grad_out, conv_weight, pre_act, down_weight):
    padded = with_halo(grad_out, ((SLAB, 1),), 1)
    stacked = shifted_stack(padded, NZ)
    partial_sum = lax.dot_general(
        stacked, conv_weight, (((0, 1), (0, 1)), ((), ())), preferred_element_type=jnp.float32
    )
    owned = lax.psum_scatter(
        partial_sum.astype(jnp.bfloat16), "chan", scatter_dimension=2, tiled=True
    )
    grad_act = lax.all_to_all(owned, "chan", split_axis=1, concat_axis=2, tiled=True)
    values = pre_act.astype(jnp.float32)
    grad_pre = (grad_act.astype(jnp.float32) * gelu_slope(values)).astype(jnp.bfloat16)
    result = lax.dot_general(
        grad_pre, down_weight, (((2,), (2,)), ((), ())), preferred_element_type=jnp.float32
    )
    return result.astype(jnp.bfloat16)


def piece_order(q):
    first = 2 + 2 * (q & 1)
    second = 6 - first
    return [q, q ^ first, q ^ second, q ^ 6, q ^ 1, q ^ 1 ^ second, q ^ 1 ^ first, q ^ 7]


def conv_kernel(where_ref, *refs, sources, added, planes):
    refs = list(refs)
    groups = []
    for margins, pieces in sources:
        cells_refs = refs[: 3 if margins else 1]
        del refs[: len(cells_refs)]
        groups.append((cells_refs, refs[:pieces]))
        del refs[:pieces]
    start_ref = refs.pop(0) if added else None
    out_ref = refs.pop(0)
    for n, (cells_refs, weights) in enumerate(groups):
        if len(weights) == 1:
            groups[n] = (cells_refs, weights[0])
            continue
        table = refs.pop(0)
        for piece, spot in zip(weights, piece_order(where_ref[0])):
            share = piece.shape[0]
            table[pl.ds(pl.multiple_of(spot * share, 16), share), :] = piece[...]
        groups[n] = (cells_refs, table)
    copies = refs.pop(0)

    extent, rows, width = groups[0][0][0].shape
    cells = rows - 2 * NZ
    needed = sorted({plane + step for plane in planes for step in range(3)})
    depth_at = lax.broadcasted_iota(jnp.int32, (rows, width), 0) % NZ
    inner_first = (where_ref[0] & 1) == 0
    totals = [start_ref[plane] if added else None for plane in planes]
    for cells_refs, table in groups:
        for x in needed:
            if x == 0:
                plane = jnp.where(inner_first, cells_refs[2][...], cells_refs[1][...])
            elif x == extent + 1:
                plane = jnp.where(inner_first, cells_refs[1][...], cells_refs[2][...])
            else:
                plane = cells_refs[0][x - 1]
            plane = plane.astype(jnp.float32)
            for step_z in (-1, 0, 1):
                if step_z == 1:
                    moved = jnp.where(depth_at >= 1, pltpu.roll(plane, 1, 0), 0.0)
                elif step_z == -1:
                    moved = jnp.where(depth_at < NZ - 1, pltpu.roll(plane, rows - 1, 0), 0.0)
                else:
                    moved = plane
                for step_y in (-1, 0, 1):
                    at = NZ * (1 - step_y)
                    lane = (3 * (step_y + 1) + step_z + 1) * width
                    copies[needed.index(x), :, lane : lane + width] = moved[
                        at : at + cells
                    ].astype(jnp.bfloat16)
        for step_x in (-1, 0, 1):
            left = jnp.concatenate(
                [copies[needed.index(plane + 1 - step_x)] for plane in planes], axis=0
            )
            right = table[(step_x + 1) * 9 * width : (step_x + 2) * 9 * width]
            term = jnp.dot(left, right, preferred_element_type=jnp.float32)
            for n in range(len(planes)):
                part = term[n * cells : (n + 1) * cells]
                totals[n] = part if totals[n] is None else totals[n] + part
    for n in range(len(planes)):
        out_ref[n] = totals[n].astype(out_ref.dtype)


def conv_blocks(where, sources, start, planes, kind, part=1):
    extent, rows, width = sources[0][0][0].shape
    wide = sources[0][1][0].shape[1]
    table_rows = sum(v.shape[0] for v in sources[0][1])
    cells = rows - 2 * NZ
    needed = len({plane + step for plane in planes for step in range(3)})
    pieces = max(len(v[1]) for v in sources)
    in_specs = [pl.BlockSpec(memory_space=pltpu.SMEM)]
    operands = [where]
    on_chip = pl.BlockSpec(memory_space=pltpu.VMEM)
    for cells_and_margins, weights in sources:
        in_specs += [on_chip] * (len(cells_and_margins) + len(weights))
        operands += [*cells_and_margins, *weights]
    if start is not None:
        in_specs.append(on_chip)
        operands.append(start)
    shape = (len(planes), cells, wide)
    out_shape = [jax.ShapeDtypeStruct(shape, kind)]
    scratch = [pltpu.VMEM((needed, cells, 9 * width), jnp.bfloat16)]
    if pieces > 1:
        out_shape.append(jax.ShapeDtypeStruct((table_rows, wide), jnp.bfloat16))
    return pl.pallas_call(
        functools.partial(
            conv_kernel,
            sources=[(len(v[0]) > 1, len(v[1])) for v in sources],
            added=start is not None,
            planes=planes,
        ),
        in_specs=in_specs,
        out_specs=[on_chip] * len(out_shape),
        out_shape=out_shape,
        scratch_shapes=scratch,
        compiler_params=pltpu.CompilerParams(vmem_limit_bytes=LIMIT * 2**20),
        cost_estimate=pl.CostEstimate(
            flops=2 * math.prod(shape) * table_rows * len(sources) // part,
            transcendentals=0,
            bytes_accessed=(2 * math.prod(shape) + 2 * table_rows * wide * len(sources)) // part,
        ),
        name="conv_blocks",
    )(*operands)


def down_kernel(mine_ref, theirs_ref, slope_ref, weight_ref, *refs, first, step):
    out_ref = refs[-1]
    at = pl.program_id(0)
    plane = first + step * at
    act = (mine_ref[plane] + theirs_ref[at].astype(jnp.float32)).astype(jnp.bfloat16)
    pre = (act.astype(jnp.float32) * slope_ref[plane]).astype(jnp.bfloat16)
    grown = [
        lax.dot_general(
            pre,
            weight_ref[e],
            (((1,), (1,)), ((), ())),
            preferred_element_type=jnp.float32,
        ).astype(out_ref.dtype)
        for e in range(weight_ref.shape[0])
    ]
    out_ref[0] = jnp.swapaxes(jnp.stack(grown), 0, 1)


def down_blocks(mine, theirs, slope, weight, planes, partly):
    extent, cells, wide = slope.shape
    offsets, fine, _ = weight.shape
    first = planes[0]
    step = planes[1] - first if len(planes) > 1 else 0
    on_chip = pl.BlockSpec(memory_space=pltpu.VMEM)
    in_specs = [on_chip] * 4
    operands = [mine, theirs, slope, weight]
    if partly is not None:
        in_specs.append(pl.BlockSpec(memory_space=pl.ANY))
        operands.append(partly)
    return pl.pallas_call(
        functools.partial(down_kernel, first=first, step=step),
        grid=(len(planes),),
        in_specs=in_specs,
        out_specs=pl.BlockSpec(
            (1, cells, offsets, fine), lambda i: (first + step * i, 0, 0, 0)
        ),
        out_shape=jax.ShapeDtypeStruct((extent, cells, offsets, fine), jnp.bfloat16),
        input_output_aliases={} if partly is None else {4: 0},
        compiler_params=pltpu.CompilerParams(vmem_limit_bytes=20 * 2**20),
        cost_estimate=pl.CostEstimate(
            flops=2 * len(planes) * cells * wide * offsets * fine,
            transcendentals=0,
            bytes_accessed=len(planes) * cells * (wide * 10 + offsets * fine * 2),
        ),
        name="down_blocks",
    )(*operands)


def planar_moves(swap):
    return [(q, swap(q)) for q in range(8)]


def two_level_body(grad_out, conv_weight, pre_act, down_weight):
    width, extent, plane = grad_out.shape
    taps, _, wide = conv_weight.shape
    block = plane // 4
    k = lax.axis_index("chan")
    q = lax.axis_index(PLANAR)
    far = [(i, i ^ 2) for i in range(4)]
    near = [(i, i ^ 1) for i in range(4)]
    first = planar_moves(lambda d: d ^ (2 if d & 1 == 0 else 4))
    second = planar_moves(lambda d: d ^ (4 if d & 1 == 0 else 2))
    other = [(0, 1), (1, 0)]
    middle = [(1, 2), (2, 1)]

    def after(value, *others):
        return lax.optimization_barrier((value, *others))[0]

    def margins(part):
        head, tail = part[:, :1], part[:, extent - 1 :]
        inner = lax.ppermute(
            jnp.where(lax.axis_index("pair") == 0, tail, head), "pair", other
        )
        outer = lax.ppermute(
            jnp.where(lax.axis_index("space") == 0, tail, head), SLAB, middle
        )
        return inner, outer

    table = conv_weight.reshape(taps * width, wide)
    share = taps * width // 8
    piece = lax.dynamic_slice_in_dim(table, q * share, share, 0)
    got = lax.ppermute(piece, "chan", far)

    cells = jnp.pad(
        jnp.transpose(after(grad_out, piece), (1, 2, 0)), ((0, 0), (NZ, NZ), (0, 0))
    )

    def window(which):
        return lax.dynamic_slice_in_dim(cells, which * block, block + 2 * NZ, 1)

    where = jnp.reshape(q, (1,)).astype(jnp.int32)
    own_one, own_two = window(k ^ 1), window(k)
    own_inner, own_outer = margins(jnp.stack([own_one, own_two]))
    every = (0, 1, 2, 3)
    begun, kept = [
        conv_blocks(
            where,
            [((cells_of, own_inner[n, 0], own_outer[n, 0]), [table])],
            None,
            every,
            jnp.float32,
            PART[0],
        )[0]
        for n, cells_of in enumerate((own_one, own_two))
    ]
    slope = gelu_slope(after(pre_act, piece).astype(jnp.float32))
    got, window_one, window_two = lax.optimization_barrier(
        (got, window(k ^ 3), window(k ^ 2), begun, kept, slope)
    )[:3]
    far_one = lax.ppermute(window_one, "chan", far)
    got_a = lax.ppermute(got, PLANAR, first)
    got_b = lax.ppermute(got, PLANAR, second)
    got_c = lax.ppermute(got_a, PLANAR, second)
    pair_got, pair_a = [lax.ppermute(v, "pair", other) for v in (got, got_a)]
    got_b = after(got_b, far_one)
    pair_b = lax.ppermute(got_b, "pair", other)
    far_two = lax.ppermute(after(window_two, far_one), "chan", far)
    one_inner, one_outer = margins(far_one[None])
    got_c, pair_got, pair_a, one_outer = lax.optimization_barrier(
        (got_c, pair_got, pair_a, one_outer)
    )
    pair_c = lax.ppermute(got_c, "pair", other)
    pieces = [got, got_a, got_b, got_c, pair_got, pair_a, pair_b, pair_c]

    sent, far_table = conv_blocks(
        where, [((far_one,), pieces)], begun, GROUPS[0], jnp.bfloat16, PART[1]
    )
    theirs = [lax.ppermute(sent, "chan", near)]
    for planes in GROUPS[1:]:
        far_one = after(far_one, sent)
        one = (far_one, one_inner[0, 0], one_outer[0, 0])
        sent = conv_blocks(
            where, [(one, [far_table])], begun, planes, jnp.bfloat16, PART[2]
        )[0]
        theirs.append(lax.ppermute(sent, "chan", near))
    far_two = after(far_two, sent)
    two_inner, two_outer = margins(far_two[None])
    two = (far_two, two_inner[0, 0], two_outer[0, 0])
    kept = conv_blocks(where, [(two, [far_table])], kept, every, jnp.float32, PART[3])[0]
    result = None
    for planes, part in zip(GROUPS, theirs):
        result = down_blocks(kept, part, slope, down_weight, planes, result)
    return result


def solution(mesh):
    sizes = dict(mesh.shape)
    four = sizes["chan"] == 4 and all(sizes[axis] == 2 for axis in PLANAR)

    def run(grad_out, conv_weight, pre_act, down_weight):
        split = grad_out.shape[0] // sizes["chan"]
        body = two_level_body if four and split == 128 and grad_out.shape[1] == 32 else general_body
        in_specs = (
            P("chan", ("groups", "space", "pair"), None),
            P(None, "chan", None),
            P(("groups", "space", "pair"), "chan", None),
            P(),
        )
        out_specs = P(("groups", "space", "pair"), "chan", None, None)
        return jax.shard_map(
            body, mesh=mesh, in_specs=in_specs, out_specs=out_specs, check_vma=False
        )(grad_out, conv_weight, pre_act, down_weight)

    return run
```
